32 devices in a mesh: tm: 32 (over z, y, x, core).
Axes of the slice: x: 2, y: 2, z: 4, core: 2. Of those that a mesh axis runs over, the one named last changes fastest.
Arguments:
- wrapped: float32 [4096, 3, 512], P('tm'), may hold values from 0 to 1, as said below
- crossings: int32 [4096, 3, 512], P('tm'), may hold values from -1 to 1, as said below
- box_size: float32 [3], replicated, may hold values from 4 to 12
Outputs:
- msd: float32 [512, 128], P('tm')
The draws below stay inside these ranges and needn't reach their ends.
Inputs may be any that keep to these rules, and one draw needn't show every extreme that they name: `wrapped`: scaled coordinates within the unit cell. per-frame crossings, one of -1, 0, 1; most entries are 0.
All inputs are finite; a program needn't handle non-finite values.
Results may differ from the reference program's by a relative error of at most 0.0003.
Values sent between devices are 32-bit elements; how exact they have to be, the bound alone decides.
A program may use at most 64 MiB of HBM per device.

```python
import math
import jax
import jax.numpy as jnp
from jax import lax

ATOMS = 512
LAGS = 128
NT = 4096


def draw_wrapped(key, part):
    base_key, jitter_key = jax.random.split(jax.random.fold_in(key, 11))
    base = jax.random.uniform(base_key, (1, 3, ATOMS), jnp.float32)
    jitter = 0.08 * jax.random.normal(jitter_key, (NT, 3, ATOMS), jnp.float32)
    return jnp.mod(base + jitter, 1.0)


def draw_crossings(key, part):
    rolls = jax.random.randint(jax.random.fold_in(key, 23), (NT, 3, ATOMS), 0, 256, dtype=jnp.int32)
    upward = jnp.where(rolls == 0, 1, 0).astype(jnp.int32)
    downward = jnp.where(rolls == 255, 1, 0).astype(jnp.int32)
    return upward - downward


def setup_inputs(seed: int = 0) -> dict:
    key_list = jax.random.split(jax.random.key(seed), 4)
    wrapped = draw_wrapped(jax.random.fold_in(key_list[3], 71), 0)
    crossings = draw_crossings(jax.random.fold_in(key_list[3], 71), 0)
    box_size = jnp.clip(jnp.exp(jax.random.uniform(key_list[2], (3,), jnp.float32, math.log(4.0), math.log(12.0))), 4.0, 12.0)
    return {"wrapped": wrapped, "crossings": crossings, "box_size": box_size}


def reference(wrapped, crossings, box_size):
    image = jnp.cumsum(crossings, axis=0)
    unwrapped = (wrapped + image.astype(jnp.float32)) * box_size[None, :, None]
    total_frames = unwrapped.shape[0]
    atom_count = unwrapped.shape[2]
    frame_ids = jnp.arange(total_frames, dtype=jnp.int32)

    def per_block(first_atom):
        block = lax.dynamic_slice_in_dim(unwrapped, first_atom, 128, 2)
        extended = jnp.concatenate([block, jnp.zeros((LAGS, 3, 128), jnp.float32)], axis=0)

        def per_lag(lag_step):
            window = lax.dynamic_slice_in_dim(extended, lag_step, total_frames, 0)
            moved = window - block
            squares = jnp.sum(moved * moved, axis=1)
            in_range = (frame_ids + lag_step) < total_frames
            return jnp.sum(jnp.where(in_range[:, None], squares, jnp.float32(0.0)), axis=0)

        return lax.map(per_lag, jnp.arange(LAGS, dtype=jnp.int32))

    parts = lax.map(per_block, jnp.arange(atom_count // 128, dtype=jnp.int32) * 128)
    lag_sum = jnp.transpose(parts, (1, 0, 2)).reshape(LAGS, atom_count)
    divisor = (total_frames - jnp.arange(LAGS, dtype=jnp.int32)).astype(jnp.float32)
    return (lag_sum / divisor[:, None]).T
```

```python
import functools

import jax
import jax.numpy as jnp
from jax import lax
from jax.experimental import pallas as pl
from jax.experimental.pallas import tpu as pltpu
from jax.sharding import PartitionSpec as P

LAGS = 128
LANES = 128
SUB = 8
MESH = pl.DeviceIdType.MESH


def kernel(n, wrapped, crossings, box, out, wbuf, xbuf, sbuf, hbuf, mean_buf, delta_buf,
           ext, sq, lagbuf, tbuf, rbuf, load_sem, halo_send, halo_recv, part_send, part_recv):
    dims, depth = wbuf.shape[0], wbuf.shape[1]
    frames = SUB * depth
    groups = sbuf.shape[0]
    per_owner = out.shape[0]
    owners = LANES // per_owner
    me = lax.axis_index("tm")
    is_last = me == n - 1
    prev = lax.rem(me + n - 1, n)
    nxt = lax.rem(me + 1, n)

    def load(i, which):
        c, s = i // SUB, lax.rem(i, SUB)
        src, dst = ((wrapped, wbuf), (crossings, xbuf))[which]
        return pltpu.make_async_copy(src.at[s, :, c, :], dst.at[c, :, s, :], load_sem.at[which, i])

    @pl.loop(0, dims * SUB)
    def _(i):
        load(i, 0).start()
        load(i, 1).start()

    barrier = pltpu.get_barrier_semaphore()

    @pl.loop(1, n)
    def _(o):
        pl.semaphore_signal(barrier, inc=1, device_id=(lax.rem(me + o, n),), device_id_type=MESH)

    @pl.loop(0, dims * SUB)
    def _(i):
        load(i, 0).wait()
        load(i, 1).wait()

    sub_ids = lax.broadcasted_iota(jnp.int32, (SUB, LANES), 0)

    def halo(i):
        return pltpu.make_async_remote_copy(
            src_ref=sbuf.at[i // dims, lax.rem(i, dims)],
            dst_ref=hbuf.at[i // dims, lax.rem(i, dims)],
            send_sem=halo_send.at[i], recv_sem=halo_recv.at[i],
            device_id=(prev,), device_id_type=MESH)

    def first_group(device):
        return device * groups // n + 1

    def prepare(step):
        g = lax.rem(step // dims + first_group(prev), groups)
        c = lax.rem(step, dims)
        lanes = pl.ds(pl.multiple_of(g * LANES, LANES), LANES)
        box_len = box[c]
        counts = [xbuf[c, 0, :, lanes].astype(jnp.float32)]
        for r in range(1, depth):
            counts.append(counts[-1] + xbuf[c, r, :, lanes].astype(jnp.float32))
        incl = counts[-1]
        for shift in (1, 2, 4):
            incl = incl + jnp.where(sub_ids >= shift, pltpu.roll(incl, shift, 0), 0.0)
        total = jnp.broadcast_to(incl[SUB - 1:SUB, :], (SUB, LANES))
        before = incl - counts[-1]
        tot_pos = jnp.zeros((SUB, LANES), jnp.float32)
        for r in range(depth):
            pos = (wbuf[c, r, :, lanes] + (counts[r] + before)) * box_len
            sbuf[g, c, r] = pos
            tot_pos = tot_pos + pos
        mean = jnp.broadcast_to(jnp.sum(tot_pos, axis=0, keepdims=True), (SUB, LANES)) * (1.0 / frames)
        mean_buf[g, c] = mean
        delta_buf[g, c] = total * box_len - mean
        return g * dims + c

    pl.semaphore_wait(barrier, n - 1)

    @pl.loop(0, groups * dims)
    def _(step):
        i = prepare(step)

        @pl.when(me > 0)
        def _():
            halo(i).start()

    end_row = jnp.where(is_last, SUB, 4 * SUB)

    def part(g, d):
        owner = g * owners + d
        return owner, pltpu.make_async_remote_copy(
            src_ref=tbuf.at[owner], dst_ref=rbuf.at[me],
            send_sem=part_send.at[owner], recv_sem=part_recv.at[me],
            device_id=(owner,), device_id_type=MESH)

    @pl.loop(0, groups)
    def _(gi):
        g = lax.rem(gi + first_group(me), groups)

        @pl.loop(0, LAGS)
        def _(k):
            lagbuf[pl.ds(pl.multiple_of(k * SUB, SUB), SUB), :] = jnp.zeros((SUB, LANES), jnp.float32)

        sq[...] = jnp.zeros_like(sq)

        @pl.loop(0, dims)
        def _(c):
            mean, delta = mean_buf[g, c], delta_buf[g, c]
            for r in range(depth):
                own = sbuf[g, c, r] - mean
                ext[r, 0:SUB, :] = own
                sq[r, 0:SUB, :] = sq[r, 0:SUB, :] + own * own

            @pl.when(is_last)
            def _():
                for r in range(depth):
                    ext[r, SUB:2 * SUB, :] = jnp.zeros((SUB, LANES), jnp.float32)

            @pl.when(jnp.logical_not(is_last))
            def _():
                halo(g * dims + c).wait_recv()
                for r in range(depth):
                    far = hbuf[g, c, r] + delta
                    ext[r, SUB:2 * SUB, :] = far
                    sq[r, SUB:2 * SUB, :] = sq[r, SUB:2 * SUB, :] + far * far

            @pl.loop(0, LAGS // depth)
            def _(q):
                near = [ext[r, 0:SUB, :] * -2.0 for r in range(depth)]
                rows = [pl.ds(pl.multiple_of((q * depth + j) * SUB, SUB), SUB) for j in range(depth)]
                acc = [None] * depth
                for m in range(2 * depth - 1):
                    far = ext[m % depth, pl.ds(q + m // depth, SUB), :]
                    for r in range(max(0, m - depth + 1), min(depth - 1, m) + 1):
                        j = m - r
                        term = far * near[r]
                        acc[j] = term if acc[j] is None else acc[j] + term
                        if r == depth - 1:
                            lagbuf[rows[j], :] = lagbuf[rows[j], :] + acc[j]

        own_total = sq[0, 0:SUB, :]
        for r in range(1, depth):
            own_total = own_total + sq[r, 0:SUB, :]

        @pl.loop(0, LAGS // depth)
        def _(q):
            row = sub_ids + q
            near_sum = own_total
            far_sum = sq[0, pl.ds(q, SUB), :]
            for r in range(1, depth):
                far_sum = far_sum + sq[r, pl.ds(q, SUB), :]
            for j in range(depth):
                base = jnp.where(row >= end_row, 0.0, jnp.where(row == end_row - 1, near_sum, own_total))
                rows = pl.ds(pl.multiple_of((q * depth + j) * SUB, SUB), SUB)
                lagbuf[rows, :] = lagbuf[rows, :] + (base + far_sum)
                if j < depth - 1:
                    near_sum = near_sum - sq[depth - 1 - j, 0:SUB, :]
                    far_sum = far_sum + (sq[j, pl.ds(q + 1, SUB), :] - sq[j, pl.ds(q, SUB), :])

        blocks = []
        for kb in range(LAGS // SUB):
            val = lagbuf[pl.ds(kb * SUB * SUB, SUB, stride=SUB), :]
            for s in range(1, SUB):
                val = val + lagbuf[pl.ds(kb * SUB * SUB + s, SUB, stride=SUB), :]
            blocks.append(val)
        by_atom = jnp.concatenate(blocks, axis=0).T
        for d in range(owners):
            tbuf[g * owners + d] = by_atom[d * per_owner:(d + 1) * per_owner, :]

        @pl.loop(0, owners)
        def _(d):
            owner, copy = part(g, d)

            @pl.when(owner != me)
            def _():
                copy.start()

    out[...] = tbuf[me]

    @pl.loop(1, n)
    def _(o):
        src = lax.rem(me + o, n)
        pltpu.make_async_remote_copy(
            src_ref=tbuf.at[src], dst_ref=rbuf.at[src],
            send_sem=part_send.at[src], recv_sem=part_recv.at[src],
            device_id=(src,), device_id_type=MESH).wait()
        out[...] = out[...] + rbuf[src]

    lag_ids = lax.broadcasted_iota(jnp.int32, (per_owner, LAGS), 1)
    out[...] = out[...] / (n * frames - lag_ids).astype(jnp.float32)

    @pl.when(me > 0)
    def _():
        @pl.loop(0, groups * dims)
        def _(i):
            halo(i).wait_send()


def on_device(n, wrapped, crossings, box_size):
    frames, dims, atoms = wrapped.shape
    depth, groups = frames // SUB, atoms // LANES
    per_owner = atoms // n
    assert frames == LAGS and atoms % LANES == 0 and LANES % per_owner == 0
    split = (SUB, depth, dims, atoms)
    any_spec = pl.BlockSpec(memory_space=pl.ANY)
    f32 = jnp.float32
    return pl.pallas_call(
        functools.partial(kernel, n),
        out_shape=jax.ShapeDtypeStruct((per_owner, LAGS), f32),
        in_specs=[any_spec, any_spec, pl.BlockSpec(memory_space=pltpu.SMEM)],
        out_specs=pl.BlockSpec(memory_space=pltpu.VMEM),
        scratch_shapes=[
            pltpu.VMEM((dims, depth, SUB, atoms), f32),
            pltpu.VMEM((dims, depth, SUB, atoms), jnp.int32),
            pltpu.VMEM((groups, dims, depth, SUB, LANES), f32),
            pltpu.VMEM((groups, dims, depth, SUB, LANES), f32),
            pltpu.VMEM((groups, dims, SUB, LANES), f32),
            pltpu.VMEM((groups, dims, SUB, LANES), f32),
            pltpu.VMEM((depth, 2 * SUB, LANES), f32),
            pltpu.VMEM((depth, 2 * SUB, LANES), f32),
            pltpu.VMEM((LAGS * SUB, LANES), f32),
            pltpu.VMEM((n, per_owner, LAGS), f32),
            pltpu.VMEM((n, per_owner, LAGS), f32),
            pltpu.SemaphoreType.DMA((2, dims * SUB)),
            pltpu.SemaphoreType.DMA((groups * dims,)),
            pltpu.SemaphoreType.DMA((groups * dims,)),
            pltpu.SemaphoreType.DMA((n,)),
            pltpu.SemaphoreType.DMA((n,)),
        ],
        compiler_params=pltpu.CompilerParams(collective_id=0, has_side_effects=True),
    )(wrapped.reshape(split), crossings.reshape(split), box_size)


def solution(mesh):
    in_specs = (P("tm", None, None), P("tm", None, None), P())
    out_specs = P("tm", None)
    return jax.shard_map(
        functools.partial(on_device, mesh.shape["tm"]), mesh=mesh,
        in_specs=in_specs, out_specs=out_specs, check_vma=False)
```

```python
import functools

import jax
import jax.numpy as jnp
from jax import lax
from jax.experimental import pallas as pl
from jax.experimental.pallas import tpu as pltpu
from jax.sharding import PartitionSpec as P

LAGS = 128
LANES = 128
SUB = 8
MESH = pl.DeviceIdType.MESH


def kernel(n, wrapped, crossings, box, out, wbuf, xbuf, sbuf, hbuf, mean_buf, delta_buf,
           ext, sq, lagbuf, tbuf, rbuf, load_sem, halo_send, halo_recv, part_send, part_recv):
    dims, groups, frames = wbuf.shape[:3]
    depth = frames // SUB
    per_owner = out.shape[0]
    owners = LANES // per_owner
    me = lax.axis_index("tm")
    is_last = me == n - 1
    prev = lax.rem(me + n - 1, n)
    nxt = lax.rem(me + 1, n)

    def load(i, which):
        c, g = i // groups, lax.rem(i, groups)
        lanes = pl.ds(pl.multiple_of(g * LANES, LANES), LANES)
        src, dst = ((wrapped, wbuf), (crossings, xbuf))[which]
        return pltpu.make_async_copy(src.at[c, :, lanes], dst.at[c, g], load_sem.at[which, i])

    @pl.loop(0, dims * groups)
    def _(i):
        load(i, 0).start()
        load(i, 1).start()

    barrier = pltpu.get_barrier_semaphore()

    @pl.loop(1, n)
    def _(o):
        pl.semaphore_signal(barrier, inc=1, device_id=(lax.rem(me + o, n),), device_id_type=MESH)

    @pl.loop(0, dims * groups)
    def _(i):
        load(i, 0).wait()
        load(i, 1).wait()

    sub_ids = lax.broadcasted_iota(jnp.int32, (SUB, LANES), 0)

    def halo(i):
        return pltpu.make_async_remote_copy(
            src_ref=sbuf.at[i // dims, lax.rem(i, dims)],
            dst_ref=hbuf.at[i // dims, lax.rem(i, dims)],
            send_sem=halo_send.at[i], recv_sem=halo_recv.at[i],
            device_id=(prev,), device_id_type=MESH)

    def first_group(device):
        return device * groups // n + 1

    def prepare(step):
        g = lax.rem(step // dims + first_group(prev), groups)
        c = lax.rem(step, dims)
        box_len = box[c]
        counts = [xbuf[c, g, pl.ds(0, SUB, stride=depth), :].astype(jnp.float32)]
        for r in range(1, depth):
            counts.append(counts[-1] + xbuf[c, g, pl.ds(r, SUB, stride=depth), :].astype(jnp.float32))
        incl = counts[-1]
        for shift in (1, 2, 4):
            incl = incl + jnp.where(sub_ids >= shift, pltpu.roll(incl, shift, 0), 0.0)
        total = jnp.broadcast_to(incl[SUB - 1:SUB, :], (SUB, LANES))
        before = incl - counts[-1]
        tot_pos = jnp.zeros((SUB, LANES), jnp.float32)
        for r in range(depth):
            pos = (wbuf[c, g, pl.ds(r, SUB, stride=depth), :] + (counts[r] + before)) * box_len
            sbuf[g, c, r] = pos
            tot_pos = tot_pos + pos
        mean = jnp.broadcast_to(jnp.sum(tot_pos, axis=0, keepdims=True), (SUB, LANES)) * (1.0 / frames)
        mean_buf[g, c] = mean
        delta_buf[g, c] = total * box_len - mean
        return g * dims + c

    pl.semaphore_wait(barrier, n - 1)

    @pl.loop(0, groups * dims)
    def _(step):
        i = prepare(step)

        @pl.when(me > 0)
        def _():
            halo(i).start()

    end_row = jnp.where(is_last, SUB, 4 * SUB)

    def part(g, d):
        owner = g * owners + d
        return owner, pltpu.make_async_remote_copy(
            src_ref=tbuf.at[owner], dst_ref=rbuf.at[me],
            send_sem=part_send.at[owner], recv_sem=part_recv.at[me],
            device_id=(owner,), device_id_type=MESH)

    @pl.loop(0, groups)
    def _(gi):
        g = lax.rem(gi + first_group(me), groups)

        @pl.loop(0, LAGS)
        def _(k):
            lagbuf[pl.ds(pl.multiple_of(k * SUB, SUB), SUB), :] = jnp.zeros((SUB, LANES), jnp.float32)

        sq[...] = jnp.zeros_like(sq)

        @pl.loop(0, dims)
        def _(c):
            mean, delta = mean_buf[g, c], delta_buf[g, c]
            for r in range(depth):
                own = sbuf[g, c, r] - mean
                ext[r, 0:SUB, :] = own
                sq[r, 0:SUB, :] = sq[r, 0:SUB, :] + own * own

            @pl.when(is_last)
            def _():
                for r in range(depth):
                    ext[r, SUB:2 * SUB, :] = jnp.zeros((SUB, LANES), jnp.float32)

            @pl.when(jnp.logical_not(is_last))
            def _():
                halo(g * dims + c).wait_recv()
                for r in range(depth):
                    far = hbuf[g, c, r] + delta
                    ext[r, SUB:2 * SUB, :] = far
                    sq[r, SUB:2 * SUB, :] = sq[r, SUB:2 * SUB, :] + far * far

            @pl.loop(0, LAGS // depth)
            def _(q):
                near = [ext[r, 0:SUB, :] * -2.0 for r in range(depth)]
                rows = [pl.ds(pl.multiple_of((q * depth + j) * SUB, SUB), SUB) for j in range(depth)]
                acc = [None] * depth
                for m in range(2 * depth - 1):
                    far = ext[m % depth, pl.ds(q + m // depth, SUB), :]
                    for r in range(max(0, m - depth + 1), min(depth - 1, m) + 1):
                        j = m - r
                        term = far * near[r]
                        acc[j] = term if acc[j] is None else acc[j] + term
                        if r == depth - 1:
                            lagbuf[rows[j], :] = lagbuf[rows[j], :] + acc[j]

        own_total = sq[0, 0:SUB, :]
        for r in range(1, depth):
            own_total = own_total + sq[r, 0:SUB, :]

        @pl.loop(0, LAGS // depth)
        def _(q):
            row = sub_ids + q
            near_sum = own_total
            far_sum = sq[0, pl.ds(q, SUB), :]
            for r in range(1, depth):
                far_sum = far_sum + sq[r, pl.ds(q, SUB), :]
            for j in range(depth):
                base = jnp.where(row >= end_row, 0.0, jnp.where(row == end_row - 1, near_sum, own_total))
                rows = pl.ds(pl.multiple_of((q * depth + j) * SUB, SUB), SUB)
                lagbuf[rows, :] = lagbuf[rows, :] + (base + far_sum)
                if j < depth - 1:
                    near_sum = near_sum - sq[depth - 1 - j, 0:SUB, :]
                    far_sum = far_sum + (sq[j, pl.ds(q + 1, SUB), :] - sq[j, pl.ds(q, SUB), :])

        blocks = []
        for kb in range(LAGS // SUB):
            val = lagbuf[pl.ds(kb * SUB * SUB, SUB, stride=SUB), :]
            for s in range(1, SUB):
                val = val + lagbuf[pl.ds(kb * SUB * SUB + s, SUB, stride=SUB), :]
            blocks.append(val)
        by_atom = jnp.concatenate(blocks, axis=0).T
        for d in range(owners):
            tbuf[g * owners + d] = by_atom[d * per_owner:(d + 1) * per_owner, :]

        @pl.loop(0, owners)
        def _(d):
            owner, copy = part(g, d)

            @pl.when(owner != me)
            def _():
                copy.start()

    out[...] = tbuf[me]

    @pl.loop(1, n)
    def _(o):
        src = lax.rem(me + o, n)
        pltpu.make_async_remote_copy(
            src_ref=tbuf.at[src], dst_ref=rbuf.at[src],
            send_sem=part_send.at[src], recv_sem=part_recv.at[src],
            device_id=(src,), device_id_type=MESH).wait()
        out[...] = out[...] + rbuf[src]

    @pl.when(me > 0)
    def _():
        @pl.loop(0, groups * dims)
        def _(i):
            halo(i).wait_send()


def on_device(n, wrapped, crossings, box_size):
    frames, dims, atoms = wrapped.shape
    depth, groups = frames // SUB, atoms // LANES
    per_owner = atoms // n
    assert frames == LAGS and atoms % LANES == 0 and LANES % per_owner == 0
    any_spec = pl.BlockSpec(memory_space=pl.ANY)
    f32 = jnp.float32
    lag_sum = pl.pallas_call(
        functools.partial(kernel, n),
        out_shape=jax.ShapeDtypeStruct((per_owner, LAGS), f32),
        in_specs=[any_spec, any_spec, pl.BlockSpec(memory_space=pltpu.SMEM)],
        out_specs=pl.BlockSpec(memory_space=pltpu.VMEM),
        scratch_shapes=[
            pltpu.VMEM((dims, groups, frames, LANES), f32),
            pltpu.VMEM((dims, groups, frames, LANES), jnp.int32),
            pltpu.VMEM((groups, dims, depth, SUB, LANES), f32),
            pltpu.VMEM((groups, dims, depth, SUB, LANES), f32),
            pltpu.VMEM((groups, dims, SUB, LANES), f32),
            pltpu.VMEM((groups, dims, SUB, LANES), f32),
            pltpu.VMEM((depth, 2 * SUB, LANES), f32),
            pltpu.VMEM((depth, 2 * SUB, LANES), f32),
            pltpu.VMEM((LAGS * SUB, LANES), f32),
            pltpu.VMEM((n, per_owner, LAGS), f32),
            pltpu.VMEM((n, per_owner, LAGS), f32),
            pltpu.SemaphoreType.DMA((2, dims * groups)),
            pltpu.SemaphoreType.DMA((groups * dims,)),
            pltpu.SemaphoreType.DMA((groups * dims,)),
            pltpu.SemaphoreType.DMA((n,)),
            pltpu.SemaphoreType.DMA((n,)),
        ],
        compiler_params=pltpu.CompilerParams(collective_id=0, has_side_effects=True),
    )(jnp.transpose(wrapped, (1, 0, 2)), jnp.transpose(crossings, (1, 0, 2)), box_size)
    divisor = (n * frames - jnp.arange(LAGS, dtype=jnp.int32)).astype(f32)
    return lag_sum / divisor[None, :]


def solution(mesh):
    in_specs = (P("tm", None, None), P("tm", None, None), P())
    out_specs = P("tm", None)
    return jax.shard_map(
        functools.partial(on_device, mesh.shape["tm"]), mesh=mesh,
        in_specs=in_specs, out_specs=out_specs, check_vma=False)
```

```python
import functools

import jax
import jax.numpy as jnp
from jax import lax
from jax.experimental import pallas as pl
from jax.experimental.pallas import tpu as pltpu
from jax.sharding import PartitionSpec as P

LAGS = 128
LANES = 128
SUB = 8
TURNS = SUB // 2 + 1
MESH = pl.DeviceIdType.MESH


def kernel(n, wrapped, crossings, box, out, wbuf, xbuf, sbuf, hbuf, mean_buf, delta_buf,
           own_ext, far_ext, inner_lag, cross_lag, sq, lagbuf, tbuf, rbuf, load_sem, halo_send, halo_recv, part_send, part_recv):
    dims, groups, frames = wbuf.shape[:3]
    depth = frames // SUB
    per_owner = out.shape[0]
    owners = LANES // per_owner
    me = lax.axis_index("tm")
    is_last = me == n - 1
    prev = lax.rem(me + n - 1, n)
    nxt = lax.rem(me + 1, n)

    def load(i, which):
        c, g = i // groups, lax.rem(i, groups)
        lanes = pl.ds(pl.multiple_of(g * LANES, LANES), LANES)
        src, dst = ((wrapped, wbuf), (crossings, xbuf))[which]
        return pltpu.make_async_copy(src.at[c, :, lanes], dst.at[c, g], load_sem.at[which, i])

    @pl.loop(0, dims * groups)
    def _(i):
        load(i, 0).start()
        load(i, 1).start()

    barrier = pltpu.get_barrier_semaphore()

    @pl.loop(1, n)
    def _(o):
        pl.semaphore_signal(barrier, inc=1, device_id=(lax.rem(me + o, n),), device_id_type=MESH)

    zero = jnp.zeros((SUB, LANES), jnp.float32)

    @pl.loop(0, groups * TURNS)
    def _(i):
        for d in range(2 * depth):
            inner_lag[i, d] = zero
            cross_lag[i, d] = zero

    @pl.loop(0, groups)
    def _(g):
        for r in range(depth):
            sq[g, r, 0:SUB, :] = zero
            sq[g, r, SUB:2 * SUB, :] = zero

    @pl.loop(0, dims * groups)
    def _(i):
        load(i, 0).wait()
        load(i, 1).wait()

    sub_ids = lax.broadcasted_iota(jnp.int32, (SUB, LANES), 0)

    def halo(i):
        return pltpu.make_async_remote_copy(
            src_ref=sbuf.at[i // dims, lax.rem(i, dims)],
            dst_ref=hbuf.at[i // dims, lax.rem(i, dims)],
            send_sem=halo_send.at[i], recv_sem=halo_recv.at[i],
            device_id=(prev,), device_id_type=MESH)

    def first_group(device):
        return device * groups // n + 1

    def prepare(step):
        g = lax.rem(step // dims + first_group(prev), groups)
        c = lax.rem(step, dims)
        box_len = box[c]
        counts = [xbuf[c, g, pl.ds(0, SUB, stride=depth), :].astype(jnp.float32)]
        for r in range(1, depth):
            counts.append(counts[-1] + xbuf[c, g, pl.ds(r, SUB, stride=depth), :].astype(jnp.float32))
        incl = counts[-1]
        for shift in (1, 2, 4):
            incl = incl + jnp.where(sub_ids >= shift, pltpu.roll(incl, shift, 0), 0.0)
        total = jnp.broadcast_to(incl[SUB - 1:SUB, :], (SUB, LANES))
        before = incl - counts[-1]
        tot_pos = jnp.zeros((SUB, LANES), jnp.float32)
        for r in range(depth):
            pos = (wbuf[c, g, pl.ds(r, SUB, stride=depth), :] + (counts[r] + before)) * box_len
            sbuf[g, c, r] = pos
            tot_pos = tot_pos + pos
        mean = jnp.broadcast_to(jnp.sum(tot_pos, axis=0, keepdims=True), (SUB, LANES)) * (1.0 / frames)
        mean_buf[g, c] = mean
        delta_buf[g, c] = total * box_len - mean
        return g * dims + c

    def correlate(near, far, buf, row, offsets):
        acc = {}
        for m in range(depth):
            moved = far(m)
            for r in range(depth):
                d = m - r
                if d in offsets:
                    term = moved * near[r]
                    acc[d] = acc[d] + term if d in acc else term
                    if m == depth - 1 or r == depth - 1:
                        buf[row, d + depth - 1] = buf[row, d + depth - 1] + acc[d]

    everything = range(1 - depth, depth)

    def inner(step):
        g = lax.rem(step // dims + first_group(me), groups)
        c = lax.rem(step, dims)
        mean = mean_buf[g, c]
        for r in range(depth):
            own = sbuf[g, c, r] - mean
            own_ext[g, c, r, 0:SUB, :] = own
            own_ext[g, c, r, SUB:2 * SUB, :] = own
            sq[g, r, 0:SUB, :] = sq[g, r, 0:SUB, :] + own * own
        near = [own_ext[g, c, r, 0:SUB, :] * -2.0 for r in range(depth)]
        correlate(near, lambda m: own_ext[g, c, m, 0:SUB, :], inner_lag, g * TURNS, range(depth))

        @pl.loop(1, TURNS)
        def _(q):
            near = [own_ext[g, c, r, 0:SUB, :] * -2.0 for r in range(depth)]
            correlate(near, lambda m: own_ext[g, c, m, pl.ds(q, SUB), :], inner_lag, g * TURNS + q, everything)

    def cross(g, c):
        delta = delta_buf[g, c]
        for r in range(depth):
            far = hbuf[g, c, r] + delta
            far_ext[r, 0:SUB, :] = far
            far_ext[r, SUB:2 * SUB, :] = far
            sq[g, r, SUB:2 * SUB, :] = sq[g, r, SUB:2 * SUB, :] + far * far
        near = [own_ext[g, c, r, 0:SUB, :] * -2.0 for r in range(depth)]
        correlate(near, lambda m: far_ext[m, 0:SUB, :], cross_lag, g * TURNS, range(1 - depth, 0))

        @pl.loop(1, TURNS)
        def _(q):
            low = sub_ids < SUB - q
            near = [jnp.where(low, own_ext[g, c, r, pl.ds(q, SUB), :], own_ext[g, c, r, 0:SUB, :]) * -2.0
                    for r in range(depth)]
            correlate(near, lambda m: jnp.where(low, far_ext[m, 0:SUB, :], far_ext[m, pl.ds(q, SUB), :]),
                      cross_lag, g * TURNS + q, everything)

    @pl.loop(0, groups * dims)
    def _(step):
        prepare(step)

    ahead = groups * dims // 2

    @pl.loop(0, ahead)
    def _(step):
        inner(step)

    pl.semaphore_wait(barrier, n - 1)

    @pl.when(me > 0)
    def _():
        @pl.loop(0, groups * dims)
        def _(step):
            halo(lax.rem(step // dims + first_group(prev), groups) * dims + lax.rem(step, dims)).start()

    @pl.loop(ahead, groups * dims)
    def _(step):
        inner(step)

    end_row = jnp.where(is_last, SUB, 4 * SUB)

    def part(g, d):
        owner = g * owners + d
        return owner, pltpu.make_async_remote_copy(
            src_ref=tbuf.at[owner], dst_ref=rbuf.at[me],
            send_sem=part_send.at[owner], recv_sem=part_recv.at[me],
            device_id=(owner,), device_id_type=MESH)

    @pl.loop(0, groups)
    def _(gi):
        g = lax.rem(gi + first_group(me), groups)

        @pl.when(jnp.logical_not(is_last))
        def _():
            @pl.loop(0, dims)
            def _(c):
                halo(g * dims + c).wait_recv()
                cross(g, c)

        def ins(q, d):
            return inner_lag[g * TURNS + q, d + depth - 1]

        def crs(q, d):
            return cross_lag[g * TURNS + q, d + depth - 1]

        half = SUB // 2
        lows = [sub_ids < SUB - q for q in range(TURNS)]
        for k in range(LAGS):
            q, j = k // depth, k % depth
            if q == 0:
                val = ins(0, j)
            elif q <= half:
                val = jnp.where(lows[q], ins(q, j), crs(q, j))
            else:
                val = jnp.where(lows[SUB - q], crs(SUB - q, j), ins(SUB - q, -j))
            if j > 0:
                if q < half:
                    val = val + jnp.where(lows[q + 1], ins(q + 1, j - depth), crs(q + 1, j - depth))
                elif q < SUB - 1:
                    p = SUB - 1 - q
                    val = val + jnp.where(lows[p], crs(p, j - depth), ins(p, depth - j))
                else:
                    val = val + crs(0, j - depth)
            lagbuf[k * SUB:(k + 1) * SUB, :] = val

        own_total = sq[g, 0, 0:SUB, :]
        for r in range(1, depth):
            own_total = own_total + sq[g, r, 0:SUB, :]

        @pl.loop(0, LAGS // depth)
        def _(q):
            row = sub_ids + q
            near_sum = own_total
            far_sum = sq[g, 0, pl.ds(q, SUB), :]
            for r in range(1, depth):
                far_sum = far_sum + sq[g, r, pl.ds(q, SUB), :]
            for j in range(depth):
                base = jnp.where(row >= end_row, 0.0, jnp.where(row == end_row - 1, near_sum, own_total))
                rows = pl.ds(pl.multiple_of((q * depth + j) * SUB, SUB), SUB)
                lagbuf[rows, :] = lagbuf[rows, :] + (base + far_sum)
                if j < depth - 1:
                    near_sum = near_sum - sq[g, depth - 1 - j, 0:SUB, :]
                    far_sum = far_sum + (sq[g, j, pl.ds(q + 1, SUB), :] - sq[g, j, pl.ds(q, SUB), :])

        blocks = []
        for kb in range(LAGS // SUB):
            val = lagbuf[pl.ds(kb * SUB * SUB, SUB, stride=SUB), :]
            for s in range(1, SUB):
                val = val + lagbuf[pl.ds(kb * SUB * SUB + s, SUB, stride=SUB), :]
            blocks.append(val)
        by_atom = jnp.concatenate(blocks, axis=0).T
        for d in range(owners):
            tbuf[g * owners + d] = by_atom[d * per_owner:(d + 1) * per_owner, :]

        @pl.loop(0, owners)
        def _(d):
            owner, copy = part(g, d)

            @pl.when(owner != me)
            def _():
                copy.start()

    out[...] = tbuf[me]

    @pl.loop(1, n)
    def _(o):
        src = lax.rem(me + o, n)
        pltpu.make_async_remote_copy(
            src_ref=tbuf.at[src], dst_ref=rbuf.at[src],
            send_sem=part_send.at[src], recv_sem=part_recv.at[src],
            device_id=(src,), device_id_type=MESH).wait()
        out[...] = out[...] + rbuf[src]

    @pl.when(me > 0)
    def _():
        @pl.loop(0, groups * dims)
        def _(i):
            halo(i).wait_send()


def on_device(n, wrapped, crossings, box_size):
    frames, dims, atoms = wrapped.shape
    depth, groups = frames // SUB, atoms // LANES
    per_owner = atoms // n
    assert frames == LAGS and atoms % LANES == 0 and LANES % per_owner == 0
    any_spec = pl.BlockSpec(memory_space=pl.ANY)
    f32 = jnp.float32
    lag_sum = pl.pallas_call(
        functools.partial(kernel, n),
        out_shape=jax.ShapeDtypeStruct((per_owner, LAGS), f32),
        in_specs=[any_spec, any_spec, pl.BlockSpec(memory_space=pltpu.SMEM)],
        out_specs=pl.BlockSpec(memory_space=pltpu.VMEM),
        scratch_shapes=[
            pltpu.VMEM((dims, groups, frames, LANES), f32),
            pltpu.VMEM((dims, groups, frames, LANES), jnp.int32),
            pltpu.VMEM((groups, dims, depth, SUB, LANES), f32),
            pltpu.VMEM((groups, dims, depth, SUB, LANES), f32),
            pltpu.VMEM((groups, dims, SUB, LANES), f32),
            pltpu.VMEM((groups, dims, SUB, LANES), f32),
            pltpu.VMEM((groups, dims, depth, 2 * SUB, LANES), f32),
            pltpu.VMEM((depth, 2 * SUB, LANES), f32),
            pltpu.VMEM((groups * TURNS, 2 * depth, SUB, LANES), f32),
            pltpu.VMEM((groups * TURNS, 2 * depth, SUB, LANES), f32),
            pltpu.VMEM((groups, depth, 2 * SUB, LANES), f32),
            pltpu.VMEM((LAGS * SUB, LANES), f32),
            pltpu.VMEM((n, per_owner, LAGS), f32),
            pltpu.VMEM((n, per_owner, LAGS), f32),
            pltpu.SemaphoreType.DMA((2, dims * groups)),
            pltpu.SemaphoreType.DMA((groups * dims,)),
            pltpu.SemaphoreType.DMA((groups * dims,)),
            pltpu.SemaphoreType.DMA((n,)),
            pltpu.SemaphoreType.DMA((n,)),
        ],
        compiler_params=pltpu.CompilerParams(collective_id=0, has_side_effects=True),
    )(jnp.transpose(wrapped, (1, 0, 2)), jnp.transpose(crossings, (1, 0, 2)), box_size)
    divisor = (n * frames - jnp.arange(LAGS, dtype=jnp.int32)).astype(f32)
    return lag_sum / divisor[None, :]


def solution(mesh):
    in_specs = (P("tm", None, None), P("tm", None, None), P())
    out_specs = P("tm", None)
    return jax.shard_map(
        functools.partial(on_device, mesh.shape["tm"]), mesh=mesh,
        in_specs=in_specs, out_specs=out_specs, check_vma=False)
```

```python
import functools

import jax
import jax.numpy as jnp
from jax import lax
from jax.experimental import pallas as pl
from jax.experimental.pallas import tpu as pltpu
from jax.sharding import PartitionSpec as P

LAGS = 128
LANES = 128
SUB = 8
TURNS = SUB // 2 + 1
MESH = pl.DeviceIdType.MESH


def kernel(n, wrapped, crossings, box, out, wbuf, xbuf, sbuf, hbuf, mean_buf, delta_buf,
           own_ext, far_ext, inner_lag, cross_lag, sq, lagbuf, tbuf, rbuf, load_sem, halo_send, halo_recv, part_send, part_recv):
    dims, groups, frames = wbuf.shape[:3]
    depth = frames // SUB
    per_owner = out.shape[0]
    owners = LANES // per_owner
    me = lax.axis_index("tm")
    is_last = me == n - 1
    prev = lax.rem(me + n - 1, n)
    nxt = lax.rem(me + 1, n)

    barrier = pltpu.get_barrier_semaphore()

    @pl.loop(1, n)
    def _(o):
        pl.semaphore_signal(barrier, inc=1, device_id=(lax.rem(me + o, n),), device_id_type=MESH)

    def load(i, which):
        c, g = i // groups, lax.rem(i, groups)
        lanes = pl.ds(pl.multiple_of(g * LANES, LANES), LANES)
        src, dst = ((wrapped, wbuf), (crossings, xbuf))[which]
        return pltpu.make_async_copy(src.at[c, :, lanes], dst.at[c, g], load_sem.at[which])

    @pl.loop(0, dims * groups)
    def _(i):
        load(i, 0).start()
        load(i, 1).start()

    zero = jnp.zeros((SUB, LANES), jnp.float32)

    @pl.loop(0, groups * TURNS)
    def _(i):
        for d in range(2 * depth):
            inner_lag[i, d] = zero
            cross_lag[i, d] = zero

    @pl.loop(0, groups)
    def _(g):
        for r in range(depth):
            sq[g, r, 0:SUB, :] = zero
            sq[g, r, SUB:2 * SUB, :] = zero

    pltpu.make_async_copy(wbuf, wbuf, load_sem.at[0]).wait()
    pltpu.make_async_copy(xbuf, xbuf, load_sem.at[1]).wait()

    sub_ids = lax.broadcasted_iota(jnp.int32, (SUB, LANES), 0)

    def halo(i):
        return pltpu.make_async_remote_copy(
            src_ref=sbuf.at[i // dims, lax.rem(i, dims)],
            dst_ref=hbuf.at[i // dims, lax.rem(i, dims)],
            send_sem=halo_send, recv_sem=halo_recv.at[i],
            device_id=(prev,), device_id_type=MESH)

    def first_group(device):
        return device * groups // n + 1

    def prepare(step):
        g = lax.rem(step // dims + first_group(prev), groups)
        c = lax.rem(step, dims)
        box_len = box[c]
        counts = [xbuf[c, g, pl.ds(0, SUB, stride=depth), :].astype(jnp.float32)]
        for r in range(1, depth):
            counts.append(counts[-1] + xbuf[c, g, pl.ds(r, SUB, stride=depth), :].astype(jnp.float32))
        incl = counts[-1]
        for shift in (1, 2, 4):
            incl = incl + jnp.where(sub_ids >= shift, pltpu.roll(incl, shift, 0), 0.0)
        total = jnp.broadcast_to(incl[SUB - 1:SUB, :], (SUB, LANES))
        before = incl - counts[-1]
        tot_pos = jnp.zeros((SUB, LANES), jnp.float32)
        for r in range(depth):
            pos = (wbuf[c, g, pl.ds(r, SUB, stride=depth), :] + (counts[r] + before)) * box_len
            sbuf[g, c, r] = pos
            tot_pos = tot_pos + pos
        mean = jnp.broadcast_to(jnp.sum(tot_pos, axis=0, keepdims=True), (SUB, LANES)) * (1.0 / frames)
        mean_buf[g, c] = mean
        delta_buf[g, c] = total * box_len - mean
        return g * dims + c

    def correlate(near, far, buf, row, offsets):
        acc = {}
        for m in range(depth):
            moved = far(m)
            for r in range(depth):
                d = m - r
                if d in offsets:
                    term = moved * near[r]
                    acc[d] = acc[d] + term if d in acc else term
                    if m == depth - 1 or r == depth - 1:
                        buf[row, d + depth - 1] = buf[row, d + depth - 1] + acc[d]

    everything = range(1 - depth, depth)

    def inner(step):
        g = lax.rem(step // dims + first_group(me), groups)
        c = lax.rem(step, dims)
        mean = mean_buf[g, c]
        for r in range(depth):
            own = sbuf[g, c, r] - mean
            own_ext[g, c, r, 0:SUB, :] = own
            own_ext[g, c, r, SUB:2 * SUB, :] = own
            sq[g, r, 0:SUB, :] = sq[g, r, 0:SUB, :] + own * own
        near = [own_ext[g, c, r, 0:SUB, :] * -2.0 for r in range(depth)]
        correlate(near, lambda m: own_ext[g, c, m, 0:SUB, :], inner_lag, g * TURNS, range(depth))

        @pl.loop(1, TURNS)
        def _(q):
            near = [own_ext[g, c, r, 0:SUB, :] * -2.0 for r in range(depth)]
            correlate(near, lambda m: own_ext[g, c, m, pl.ds(q, SUB), :], inner_lag, g * TURNS + q, everything)

    def cross(g, c):
        delta = delta_buf[g, c]
        for r in range(depth):
            far = hbuf[g, c, r] + delta
            far_ext[r, 0:SUB, :] = far
            far_ext[r, SUB:2 * SUB, :] = far
            sq[g, r, SUB:2 * SUB, :] = sq[g, r, SUB:2 * SUB, :] + far * far
        near = [own_ext[g, c, r, 0:SUB, :] * -2.0 for r in range(depth)]
        correlate(near, lambda m: far_ext[m, 0:SUB, :], cross_lag, g * TURNS, range(1 - depth, 0))

        @pl.loop(1, TURNS)
        def _(q):
            low = sub_ids < SUB - q
            near = [jnp.where(low, own_ext[g, c, r, pl.ds(q, SUB), :], own_ext[g, c, r, 0:SUB, :]) * -2.0
                    for r in range(depth)]
            correlate(near, lambda m: jnp.where(low, far_ext[m, 0:SUB, :], far_ext[m, pl.ds(q, SUB), :]),
                      cross_lag, g * TURNS + q, everything)

    @pl.loop(0, groups * dims)
    def _(step):
        prepare(step)

    ahead = groups * dims // 3

    @pl.loop(0, ahead)
    def _(step):
        inner(step)

    pl.semaphore_wait(barrier, n - 1)

    @pl.when(me > 0)
    def _():
        @pl.loop(0, groups * dims)
        def _(step):
            halo(lax.rem(step // dims + first_group(prev), groups) * dims + lax.rem(step, dims)).start()

    @pl.loop(ahead, groups * dims)
    def _(step):
        inner(step)

    end_row = jnp.where(is_last, SUB, 4 * SUB)

    def part(g, d):
        owner = g * owners + d
        return owner, pltpu.make_async_remote_copy(
            src_ref=tbuf.at[owner], dst_ref=rbuf.at[me],
            send_sem=part_send, recv_sem=part_recv,
            device_id=(owner,), device_id_type=MESH)

    @pl.loop(0, groups)
    def _(gi):
        g = lax.rem(gi + first_group(me), groups)

        @pl.when(jnp.logical_not(is_last))
        def _():
            @pl.loop(0, dims)
            def _(c):
                halo(g * dims + c).wait_recv()
                cross(g, c)

        def ins(q, d):
            return inner_lag[g * TURNS + q, d + depth - 1]

        def crs(q, d):
            return cross_lag[g * TURNS + q, d + depth - 1]

        half = SUB // 2
        lows = [sub_ids < SUB - q for q in range(TURNS)]
        for k in range(LAGS):
            q, j = k // depth, k % depth
            if q == 0:
                val = ins(0, j)
            elif q <= half:
                val = jnp.where(lows[q], ins(q, j), crs(q, j))
            else:
                val = jnp.where(lows[SUB - q], crs(SUB - q, j), ins(SUB - q, -j))
            if j > 0:
                if q < half:
                    val = val + jnp.where(lows[q + 1], ins(q + 1, j - depth), crs(q + 1, j - depth))
                elif q < SUB - 1:
                    p = SUB - 1 - q
                    val = val + jnp.where(lows[p], crs(p, j - depth), ins(p, depth - j))
                else:
                    val = val + crs(0, j - depth)
            lagbuf[k * SUB:(k + 1) * SUB, :] = val

        own_total = sq[g, 0, 0:SUB, :]
        for r in range(1, depth):
            own_total = own_total + sq[g, r, 0:SUB, :]

        @pl.loop(0, LAGS // depth)
        def _(q):
            row = sub_ids + q
            near_sum = own_total
            far_sum = sq[g, 0, pl.ds(q, SUB), :]
            for r in range(1, depth):
                far_sum = far_sum + sq[g, r, pl.ds(q, SUB), :]
            for j in range(depth):
                base = jnp.where(row >= end_row, 0.0, jnp.where(row == end_row - 1, near_sum, own_total))
                rows = pl.ds(pl.multiple_of((q * depth + j) * SUB, SUB), SUB)
                lagbuf[rows, :] = lagbuf[rows, :] + (base + far_sum)
                if j < depth - 1:
                    near_sum = near_sum - sq[g, depth - 1 - j, 0:SUB, :]
                    far_sum = far_sum + (sq[g, j, pl.ds(q + 1, SUB), :] - sq[g, j, pl.ds(q, SUB), :])

        blocks = []
        for kb in range(LAGS // SUB):
            val = lagbuf[pl.ds(kb * SUB * SUB, SUB, stride=SUB), :]
            for s in range(1, SUB):
                val = val + lagbuf[pl.ds(kb * SUB * SUB + s, SUB, stride=SUB), :]
            blocks.append(val)
        by_atom = jnp.concatenate(blocks, axis=0).T
        for d in range(owners):
            tbuf[g * owners + d] = by_atom[d * per_owner:(d + 1) * per_owner, :]

        @pl.loop(0, owners)
        def _(d):
            owner, copy = part(g, d)

            @pl.when(owner != me)
            def _():
                copy.start()

    rbuf[me] = tbuf[me]
    others = pl.ds(0, n - 1)
    pltpu.make_async_remote_copy(
        src_ref=tbuf.at[others], dst_ref=rbuf.at[others], send_sem=part_send, recv_sem=part_recv,
        device_id=(nxt,), device_id_type=MESH).wait()
    out[...] = jnp.sum(rbuf[...], axis=0)

    @pl.when(me > 0)
    def _():
        pltpu.make_async_remote_copy(
            src_ref=sbuf, dst_ref=hbuf, send_sem=halo_send, recv_sem=halo_recv.at[0],
            device_id=(prev,), device_id_type=MESH).wait_send()


def on_device(n, wrapped, crossings, box_size):
    frames, dims, atoms = wrapped.shape
    depth, groups = frames // SUB, atoms // LANES
    per_owner = atoms // n
    assert frames == LAGS and atoms % LANES == 0 and LANES % per_owner == 0
    any_spec = pl.BlockSpec(memory_space=pl.ANY)
    f32 = jnp.float32
    lag_sum = pl.pallas_call(
        functools.partial(kernel, n),
        out_shape=jax.ShapeDtypeStruct((per_owner, LAGS), f32),
        in_specs=[any_spec, any_spec, pl.BlockSpec(memory_space=pltpu.SMEM)],
        out_specs=pl.BlockSpec(memory_space=pltpu.VMEM),
        scratch_shapes=[
            pltpu.VMEM((dims, groups, frames, LANES), f32),
            pltpu.VMEM((dims, groups, frames, LANES), jnp.int32),
            pltpu.VMEM((groups, dims, depth, SUB, LANES), f32),
            pltpu.VMEM((groups, dims, depth, SUB, LANES), f32),
            pltpu.VMEM((groups, dims, SUB, LANES), f32),
            pltpu.VMEM((groups, dims, SUB, LANES), f32),
            pltpu.VMEM((groups, dims, depth, 2 * SUB, LANES), f32),
            pltpu.VMEM((depth, 2 * SUB, LANES), f32),
            pltpu.VMEM((groups * TURNS, 2 * depth, SUB, LANES), f32),
            pltpu.VMEM((groups * TURNS, 2 * depth, SUB, LANES), f32),
            pltpu.VMEM((groups, depth, 2 * SUB, LANES), f32),
            pltpu.VMEM((LAGS * SUB, LANES), f32),
            pltpu.VMEM((n, per_owner, LAGS), f32),
            pltpu.VMEM((n, per_owner, LAGS), f32),
            pltpu.SemaphoreType.DMA((2,)),
            pltpu.SemaphoreType.DMA,
            pltpu.SemaphoreType.DMA((groups * dims,)),
            pltpu.SemaphoreType.DMA,
            pltpu.SemaphoreType.DMA,
        ],
        compiler_params=pltpu.CompilerParams(collective_id=0, has_side_effects=True),
    )(jnp.transpose(wrapped, (1, 0, 2)), jnp.transpose(crossings, (1, 0, 2)), box_size)
    divisor = (n * frames - jnp.arange(LAGS, dtype=jnp.int32)).astype(f32)
    return lag_sum / divisor[None, :]


def solution(mesh):
    in_specs = (P("tm", None, None), P("tm", None, None), P())
    out_specs = P("tm", None)
    return jax.shard_map(
        functools.partial(on_device, mesh.shape["tm"]), mesh=mesh,
        in_specs=in_specs, out_specs=out_specs, check_vma=False)
```

```python
import functools

import jax
import jax.numpy as jnp
from jax import lax
from jax.experimental import pallas as pl
from jax.experimental.pallas import tpu as pltpu
from jax.sharding import PartitionSpec as P

LAGS = 128
LANES = 128
SUB = 8
TURNS = SUB // 2 + 1
MESH = pl.DeviceIdType.MESH


def kernel(n, wrapped, crossings, box, out, wbuf, xbuf, sbuf, hbuf, mean_buf, delta_buf,
           own_ext, far_ext, inner_lag, cross_lag, sq, lagbuf, tbuf, rbuf, load_sem, halo_send, halo_recv, part_send, part_recv):
    dims, groups, frames = wbuf.shape[:3]
    depth = frames // SUB
    per_owner = out.shape[0]
    owners = LANES // per_owner
    me = lax.axis_index("tm")
    is_last = me == n - 1
    prev = lax.rem(me + n - 1, n)
    nxt = lax.rem(me + 1, n)

    barrier = pltpu.get_barrier_semaphore()

    @pl.loop(1, n)
    def _(o):
        pl.semaphore_signal(barrier, inc=1, device_id=(lax.rem(me + n - o, n),), device_id_type=MESH)

    def load(i, which):
        c, g = i // groups, lax.rem(i, groups)
        lanes = pl.ds(pl.multiple_of(g * LANES, LANES), LANES)
        src, dst = ((wrapped, wbuf), (crossings, xbuf))[which]
        return pltpu.make_async_copy(src.at[c, :, lanes], dst.at[c, g], load_sem.at[which])

    @pl.loop(0, dims * groups)
    def _(i):
        load(i, 0).start()
        load(i, 1).start()

    zero = jnp.zeros((SUB, LANES), jnp.float32)

    @pl.loop(0, groups * TURNS)
    def _(i):
        for d in range(2 * depth):
            inner_lag[i, d] = zero
            cross_lag[i, d] = zero

    @pl.loop(0, groups)
    def _(g):
        for r in range(depth):
            sq[g, r, 0:SUB, :] = zero
            sq[g, r, SUB:2 * SUB, :] = zero

    pltpu.make_async_copy(wbuf, wbuf, load_sem.at[0]).wait()
    pltpu.make_async_copy(xbuf, xbuf, load_sem.at[1]).wait()

    sub_ids = lax.broadcasted_iota(jnp.int32, (SUB, LANES), 0)

    def halo(i):
        return pltpu.make_async_remote_copy(
            src_ref=sbuf.at[i // dims, lax.rem(i, dims)],
            dst_ref=hbuf.at[i // dims, lax.rem(i, dims)],
            send_sem=halo_send, recv_sem=halo_recv.at[i],
            device_id=(prev,), device_id_type=MESH)

    def first_group(device):
        return device * groups // n + 1

    def prepare(step):
        g = lax.rem(step // dims + first_group(prev), groups)
        c = lax.rem(step, dims)
        box_len = box[c]
        counts = [xbuf[c, g, pl.ds(0, SUB, stride=depth), :].astype(jnp.float32)]
        for r in range(1, depth):
            counts.append(counts[-1] + xbuf[c, g, pl.ds(r, SUB, stride=depth), :].astype(jnp.float32))
        incl = counts[-1]
        for shift in (1, 2, 4):
            incl = incl + jnp.where(sub_ids >= shift, pltpu.roll(incl, shift, 0), 0.0)
        total = jnp.broadcast_to(incl[SUB - 1:SUB, :], (SUB, LANES))
        before = incl - counts[-1]
        tot_pos = jnp.zeros((SUB, LANES), jnp.float32)
        for r in range(depth):
            pos = (wbuf[c, g, pl.ds(r, SUB, stride=depth), :] + (counts[r] + before)) * box_len
            sbuf[g, c, r] = pos
            tot_pos = tot_pos + pos
        mean = jnp.broadcast_to(jnp.sum(tot_pos, axis=0, keepdims=True), (SUB, LANES)) * (1.0 / frames)
        mean_buf[g, c] = mean
        delta_buf[g, c] = total * box_len - mean
        return g * dims + c

    def correlate(near, far, buf, row, offsets):
        acc = {}
        for m in range(depth):
            moved = far(m)
            for r in range(depth):
                d = m - r
                if d in offsets:
                    term = moved * near[r]
                    acc[d] = acc[d] + term if d in acc else term
                    if m == depth - 1 or r == depth - 1:
                        buf[row, d + depth - 1] = buf[row, d + depth - 1] + acc[d]

    everything = range(1 - depth, depth)

    def inner(step):
        g = lax.rem(step // dims + first_group(me), groups)
        c = lax.rem(step, dims)
        mean = mean_buf[g, c]
        for r in range(depth):
            own = sbuf[g, c, r] - mean
            own_ext[g, c, r, 0:SUB, :] = own
            own_ext[g, c, r, SUB:2 * SUB, :] = own
            sq[g, r, 0:SUB, :] = sq[g, r, 0:SUB, :] + own * own
        near = [own_ext[g, c, r, 0:SUB, :] * -2.0 for r in range(depth)]
        correlate(near, lambda m: own_ext[g, c, m, 0:SUB, :], inner_lag, g * TURNS, range(depth))

        @pl.loop(1, TURNS)
        def _(q):
            near = [own_ext[g, c, r, 0:SUB, :] * -2.0 for r in range(depth)]
            correlate(near, lambda m: own_ext[g, c, m, pl.ds(q, SUB), :], inner_lag, g * TURNS + q, everything)

    def cross(g, c):
        delta = delta_buf[g, c]
        for r in range(depth):
            far = hbuf[g, c, r] + delta
            far_ext[r, 0:SUB, :] = far
            far_ext[r, SUB:2 * SUB, :] = far
            sq[g, r, SUB:2 * SUB, :] = sq[g, r, SUB:2 * SUB, :] + far * far
        near = [own_ext[g, c, r, 0:SUB, :] * -2.0 for r in range(depth)]
        correlate(near, lambda m: far_ext[m, 0:SUB, :], cross_lag, g * TURNS, range(1 - depth, 0))

        @pl.loop(1, TURNS)
        def _(q):
            low = sub_ids < SUB - q
            near = [jnp.where(low, own_ext[g, c, r, pl.ds(q, SUB), :], own_ext[g, c, r, 0:SUB, :]) * -2.0
                    for r in range(depth)]
            correlate(near, lambda m: jnp.where(low, far_ext[m, 0:SUB, :], far_ext[m, pl.ds(q, SUB), :]),
                      cross_lag, g * TURNS + q, everything)

    @pl.loop(0, groups * dims)
    def _(step):
        prepare(step)

    ahead = groups * dims // 3

    @pl.loop(0, ahead)
    def _(step):
        inner(step)

    pl.semaphore_wait(barrier, n - 1)

    @pl.when(me > 0)
    def _():
        @pl.loop(0, groups * dims)
        def _(step):
            halo(lax.rem(step // dims + first_group(prev), groups) * dims + lax.rem(step, dims)).start()

    @pl.loop(ahead, groups * dims)
    def _(step):
        inner(step)

    end_row = jnp.where(is_last, SUB, 4 * SUB)

    def part(g, d):
        owner = g * owners + d
        return owner, pltpu.make_async_remote_copy(
            src_ref=tbuf.at[owner], dst_ref=rbuf.at[me],
            send_sem=part_send, recv_sem=part_recv,
            device_id=(owner,), device_id_type=MESH)

    @pl.loop(0, groups)
    def _(gi):
        g = lax.rem(gi + first_group(me), groups)

        @pl.when(jnp.logical_not(is_last))
        def _():
            @pl.loop(0, dims)
            def _(c):
                halo(g * dims + c).wait_recv()
                cross(g, c)

        def ins(q, d):
            return inner_lag[g * TURNS + q, d + depth - 1]

        def crs(q, d):
            return cross_lag[g * TURNS + q, d + depth - 1]

        own_total = sq[g, 0, 0:SUB, :]
        for r in range(1, depth):
            own_total = own_total + sq[g, r, 0:SUB, :]

        half = SUB // 2
        lows = [sub_ids < SUB - q for q in range(TURNS)]
        for k in range(LAGS):
            q, j = k // depth, k % depth
            if q == 0:
                val = ins(0, j)
            elif q <= half:
                val = jnp.where(lows[q], ins(q, j), crs(q, j))
            else:
                val = jnp.where(lows[SUB - q], crs(SUB - q, j), ins(SUB - q, -j))
            if j > 0:
                if q < half:
                    val = val + jnp.where(lows[q + 1], ins(q + 1, j - depth), crs(q + 1, j - depth))
                elif q < SUB - 1:
                    p = SUB - 1 - q
                    val = val + jnp.where(lows[p], crs(p, j - depth), ins(p, depth - j))
                else:
                    val = val + crs(0, j - depth)
            if j == 0:
                row = sub_ids + q
                near_sum = own_total
                far_sum = sq[g, 0, q:q + SUB, :]
                for r in range(1, depth):
                    far_sum = far_sum + sq[g, r, q:q + SUB, :]
            else:
                near_sum = near_sum - sq[g, depth - j, 0:SUB, :]
                far_sum = far_sum + (sq[g, j - 1, q + 1:q + 1 + SUB, :] - sq[g, j - 1, q:q + SUB, :])
            base = jnp.where(row >= end_row, 0.0, jnp.where(row == end_row - 1, near_sum, own_total))
            lagbuf[k * SUB:(k + 1) * SUB, :] = val + (base + far_sum)

        blocks = []
        for kb in range(LAGS // SUB):
            val = lagbuf[pl.ds(kb * SUB * SUB, SUB, stride=SUB), :]
            for s in range(1, SUB):
                val = val + lagbuf[pl.ds(kb * SUB * SUB + s, SUB, stride=SUB), :]
            blocks.append(val)
        by_atom = jnp.concatenate(blocks, axis=0).T
        for d in range(owners):
            tbuf[g * owners + d] = by_atom[d * per_owner:(d + 1) * per_owner, :]

        @pl.loop(0, owners)
        def _(d):
            owner, copy = part(g, d)

            @pl.when(owner != me)
            def _():
                copy.start()

    rbuf[me] = tbuf[me]
    others = pl.ds(0, n - 1)
    pltpu.make_async_remote_copy(
        src_ref=tbuf.at[others], dst_ref=rbuf.at[others], send_sem=part_send, recv_sem=part_recv,
        device_id=(nxt,), device_id_type=MESH).wait()
    out[...] = jnp.sum(rbuf[...], axis=0)

    @pl.when(me > 0)
    def _():
        pltpu.make_async_remote_copy(
            src_ref=sbuf, dst_ref=hbuf, send_sem=halo_send, recv_sem=halo_recv.at[0],
            device_id=(prev,), device_id_type=MESH).wait_send()


def on_device(n, wrapped, crossings, box_size):
    frames, dims, atoms = wrapped.shape
    depth, groups = frames // SUB, atoms // LANES
    per_owner = atoms // n
    assert frames == LAGS and atoms % LANES == 0 and LANES % per_owner == 0
    any_spec = pl.BlockSpec(memory_space=pl.ANY)
    f32 = jnp.float32
    lag_sum = pl.pallas_call(
        functools.partial(kernel, n),
        out_shape=jax.ShapeDtypeStruct((per_owner, LAGS), f32),
        in_specs=[any_spec, any_spec, pl.BlockSpec(memory_space=pltpu.SMEM)],
        out_specs=pl.BlockSpec(memory_space=pltpu.VMEM),
        scratch_shapes=[
            pltpu.VMEM((dims, groups, frames, LANES), f32),
            pltpu.VMEM((dims, groups, frames, LANES), jnp.int32),
            pltpu.VMEM((groups, dims, depth, SUB, LANES), f32),
            pltpu.VMEM((groups, dims, depth, SUB, LANES), f32),
            pltpu.VMEM((groups, dims, SUB, LANES), f32),
            pltpu.VMEM((groups, dims, SUB, LANES), f32),
            pltpu.VMEM((groups, dims, depth, 2 * SUB, LANES), f32),
            pltpu.VMEM((depth, 2 * SUB, LANES), f32),
            pltpu.VMEM((groups * TURNS, 2 * depth, SUB, LANES), f32),
            pltpu.VMEM((groups * TURNS, 2 * depth, SUB, LANES), f32),
            pltpu.VMEM((groups, depth, 2 * SUB, LANES), f32),
            pltpu.VMEM((LAGS * SUB, LANES), f32),
            pltpu.VMEM((n, per_owner, LAGS), f32),
            pltpu.VMEM((n, per_owner, LAGS), f32),
            pltpu.SemaphoreType.DMA((2,)),
            pltpu.SemaphoreType.DMA,
            pltpu.SemaphoreType.DMA((groups * dims,)),
            pltpu.SemaphoreType.DMA,
            pltpu.SemaphoreType.DMA,
        ],
        compiler_params=pltpu.CompilerParams(collective_id=0, has_side_effects=True),
    )(jnp.transpose(wrapped, (1, 0, 2)), jnp.transpose(crossings, (1, 0, 2)), box_size)
    divisor = (n * frames - jnp.arange(LAGS, dtype=jnp.int32)).astype(f32)
    return lag_sum / divisor[None, :]


def solution(mesh):
    in_specs = (P("tm", None, None), P("tm", None, None), P())
    out_specs = P("tm", None)
    return jax.shard_map(
        functools.partial(on_device, mesh.shape["tm"]), mesh=mesh,
        in_specs=in_specs, out_specs=out_specs, check_vma=False)
```
